256 devices in a mesh: dp: 16 (over z, y_hi), seq: 16 (over x, y_lo, core).
Axes of the slice: x: 4, y: 4 (y_hi: 2, y_lo: 2; y = y_hi * 2 + y_lo), z: 8, core: 2. Of those that a mesh axis runs over, the one named last changes fastest.
Arguments:
- frames: bfloat16 [32, 2048, 1024], P('dp', 'seq'), may hold values from -6 to 6
- lengths: int32 [32], P('dp'), may hold values from 512 to 2048, as said below
- qkv_weight: bfloat16 [1024, 3072], P('dp'), may hold values from -8 to 8, as said below
- out_weight: bfloat16 [1024, 1024], P('dp'), may hold values from -0.75 to 0.75
- cotangent: bfloat16 [32, 2048, 1024], P('dp', 'seq'), may hold values from -6 to 6
Outputs:
- result: bfloat16 [32, 2048, 1024], P('dp', 'seq')
- frame_grad: bfloat16 [32, 2048, 1024], P('dp', 'seq')
- qkv_weight_grad: float32 [1024, 3072], P('dp')
- out_weight_grad: float32 [1024, 1024], P('dp')
The draws below stay inside these ranges and needn't reach their ends.
Inputs may be any that keep to these rules, and one draw needn't show every extreme that they name: `lengths`: valid frames of each recording; in every draw some recording is valid over the whole slab. `qkv_weight`: a projection.
All inputs are finite; a program needn't handle non-finite values.
Results may differ from the reference program's by a relative error of at most 0.023.
The reference program's roundings to bfloat16 on the way count: a program that leaves them out, or rounds other values in their place, can miss the bound.
Values may be sent and summed in bfloat16 or wider, within the bound.
No kernel may reach another device: no remote copies, remote signals or barrier semaphores. Data moves between devices by JAX's collectives and lax.ppermute only.
A program may use at most 128 MiB of HBM per device.

```python
import math
import jax
import jax.numpy as jnp
from jax import lax

D = 1024
H = 16
GROUP = 16
LEFT = 64
AHEAD = 4
FR_DEV = 128
SLAB = 2048
RECS = 32


def draw_frames(key, part):
    first_key = jax.random.fold_in(jax.random.fold_in(key, 11), 0)
    basic = jax.random.normal(first_key, (RECS, SLAB, D), jnp.float32)
    return jnp.clip(basic, -6.0, 6.0).astype(jnp.bfloat16)


def draw_lengths(key, part):
    first_key, second_key = jax.random.split(jax.random.fold_in(key, 23))
    drawn = jax.random.randint(first_key, (RECS,), SLAB // 4, SLAB + 1)
    chosen = jax.random.randint(second_key, (), 0, RECS)
    return jnp.where(jnp.arange(RECS) == chosen, SLAB, drawn).astype(jnp.int32)


def draw_qkv_weight(key, part):
    first_key = jax.random.fold_in(jax.random.fold_in(key, 37), 0)
    basic = jnp.clip(jax.random.normal(first_key, (D, 3 * D), jnp.float32), -6.0, 6.0) / jnp.sqrt(D * 1.0)
    return basic.astype(jnp.bfloat16)


def steps_of(key, shape, cuts, smallest, high):
    loudness, own = 1.0, jax.random.fold_in(key, 6)
    for dim, shards_of in cuts:
        heights = jnp.exp(jax.random.uniform(jax.random.fold_in(own, dim), (shards_of,), jnp.float32, smallest / len(cuts), high / len(cuts)))
        loudness = loudness * jnp.repeat(heights, shape[dim] // shards_of).reshape([-1 if axis == dim else 1 for axis in range(len(shape))])
    return loudness


def scatter_about(stream_key, shape, scale, most, pieces=(), held_as=jnp.bfloat16):
    entries = jax.random.normal(stream_key, shape, jnp.float32) * scale
    if len(pieces) > 0:
        entries = steps_of(stream_key, shape, pieces, -0.22, 0.18) * entries
    return jnp.clip(entries, min=-most, max=most).astype(held_as)


def setup_inputs(seed: int = 0) -> dict:
    keys = jax.random.split(jax.random.key(seed), 6)
    return {
        "frames": draw_frames(jax.random.fold_in(keys[5], 71), 0),
        "lengths": draw_lengths(jax.random.fold_in(keys[5], 71), 0),
        "qkv_weight": draw_qkv_weight(jax.random.fold_in(keys[5], 71), 0),
        "out_weight": scatter_about(keys[3], (D, D), (D // 16) ** -0.5, 0.75, ((0, 16),)),
        "cotangent": scatter_about(keys[4], (RECS, SLAB, D), 1.0, 6.0, ((0, 16), (1, 16))),
    }


def norm_rows(recording):
    as_float = recording.astype(jnp.float32)
    row_mean = lax.optimization_barrier(jnp.mean(as_float, axis=-1, keepdims=True))
    centred = as_float - row_mean
    variance = lax.optimization_barrier(jnp.mean(centred * centred, axis=-1, keepdims=True))
    inv_std = lax.rsqrt(variance + 1e-05)
    return (centred * inv_std, inv_std)

def window_mask(query_pos, key_pos, rec_length):
    group_start = query_pos // GROUP * GROUP
    inside = (key_pos[None, :] >= 0) & (key_pos[None, :] < SLAB)
    inside = inside & (key_pos[None, :] >= group_start[:, None] - LEFT)
    inside = inside & (key_pos[None, :] < group_start[:, None] + GROUP + AHEAD)
    allowed = (key_pos[None, :] < rec_length) | (query_pos[:, None] >= rec_length)
    return inside & allowed

def attend(queries, key_rows, value_rows, allowed_mask, score_scale):
    scores = jnp.einsum('fhe,khe->hfk', queries.astype(jnp.float32), key_rows.astype(jnp.float32)) * score_scale
    scores = jnp.where(allowed_mask[None], scores, -1e+30)
    row_max = lax.optimization_barrier(jnp.max(scores, axis=-1, keepdims=True))
    shifted = jnp.where(allowed_mask[None], jnp.exp(scores - row_max), 0.0)
    attn_probs = shifted / lax.optimization_barrier(jnp.sum(shifted, axis=-1, keepdims=True))
    probs_half = attn_probs.astype(jnp.bfloat16)
    mixed_rows = jnp.einsum('hfk,khe->fhe', probs_half.astype(jnp.float32), value_rows.astype(jnp.float32))
    return (mixed_rows.astype(jnp.bfloat16), attn_probs, probs_half)

def attend_back(queries, key_rows, value_rows, attn_probs, probs_half, mixed_grad, score_scale):
    value_grad = jnp.einsum('hfk,fhe->khe', probs_half.astype(jnp.float32), mixed_grad.astype(jnp.float32))
    prob_grad = jnp.einsum('fhe,khe->hfk', mixed_grad.astype(jnp.float32), value_rows.astype(jnp.float32))
    score_grad = attn_probs * (prob_grad - lax.optimization_barrier(jnp.sum(attn_probs * prob_grad, axis=-1, keepdims=True))) * score_scale
    score_grad = score_grad.astype(jnp.bfloat16).astype(jnp.float32)
    query_grad = jnp.einsum('hfk,khe->fhe', score_grad, key_rows.astype(jnp.float32))
    key_grad = jnp.einsum('hfk,fhe->khe', score_grad, queries.astype(jnp.float32))
    return (query_grad, key_grad, value_grad)

def reference(frames, lengths, qkv_weight, out_weight, cotangent):
    head_size = D // H
    span_len = FR_DEV + LEFT + AHEAD
    score_scale = 1.0 / math.sqrt(head_size)
    num_blocks = SLAB // FR_DEV

    def one_recording(totals, inputs):
        recording, rec_length, rec_cot = inputs
        centred, inv_std = norm_rows(recording)
        normed = centred.astype(jnp.bfloat16)
        projected_qkv = jnp.dot(normed, qkv_weight, preferred_element_type=jnp.float32).astype(jnp.bfloat16)
        all_queries = projected_qkv[:, :D].reshape(SLAB, H, head_size)
        key_value = jnp.pad(projected_qkv[:, D:], ((LEFT, AHEAD), (0, 0)))
        positions = jnp.arange(SLAB, dtype=jnp.int32)

        def block_inputs(block):
            first = (block * FR_DEV).astype(jnp.int32)
            queries = lax.dynamic_slice_in_dim(all_queries, first, FR_DEV, 0)
            window = lax.dynamic_slice_in_dim(key_value, first, span_len, 0)
            key_rows = window[:, :D].reshape(span_len, H, head_size)
            value_rows = window[:, D:].reshape(span_len, H, head_size)
            query_pos = first + jnp.arange(FR_DEV, dtype=jnp.int32)
            key_pos = first - LEFT + jnp.arange(span_len, dtype=jnp.int32)
            return (queries, key_rows, value_rows, window_mask(query_pos, key_pos, rec_length))

        def forward(block):
            queries, key_rows, value_rows, allowed_mask = block_inputs(block)
            mixed_rows, unused_a, unused_b = attend(queries, key_rows, value_rows, allowed_mask, score_scale)
            return mixed_rows.reshape(FR_DEV, D)
        blocks = jnp.arange(num_blocks, dtype=jnp.int32)
        mixed = lax.map(forward, blocks).reshape(SLAB, D)
        projected = jnp.dot(mixed, out_weight, preferred_element_type=jnp.float32)
        is_valid = (positions < rec_length)[:, None]
        result = jnp.where(is_valid, projected, 0.0).astype(jnp.bfloat16)
        out_grad = jnp.where(is_valid, rec_cot, jnp.zeros_like(rec_cot))
        mixed_grad = jnp.dot(out_grad, out_weight.T, preferred_element_type=jnp.float32).astype(jnp.bfloat16)

        def backward(key_acc, block):
            queries, key_rows, value_rows, allowed_mask = block_inputs(block)
            unused_m, attn_probs, probs_half = attend(queries, key_rows, value_rows, allowed_mask, score_scale)
            first = (block * FR_DEV).astype(jnp.int32)
            grad_rows = lax.dynamic_slice_in_dim(mixed_grad, first, FR_DEV, 0).reshape(FR_DEV, H, head_size)
            query_grad, key_grad, value_grad = attend_back(queries, key_rows, value_rows, attn_probs, probs_half, grad_rows, score_scale)
            piece_grad = jnp.concatenate([key_grad.reshape(span_len, D), value_grad.reshape(span_len, D)], axis=-1)
            current = lax.dynamic_slice_in_dim(key_acc, first, span_len, 0)
            key_acc = lax.dynamic_update_slice_in_dim(key_acc, current + piece_grad, first, 0)
            return (key_acc, query_grad.reshape(FR_DEV, D).astype(jnp.bfloat16))
        key_acc = jnp.zeros((SLAB + LEFT + AHEAD, 2 * D), jnp.float32)
        key_acc, query_blocks = lax.scan(backward, key_acc, blocks)
        qkv_grad = jnp.concatenate([query_blocks.reshape(SLAB, D), key_acc[LEFT:LEFT + SLAB].astype(jnp.bfloat16)], axis=-1)
        qkv_total, out_total = totals
        qkv_total = qkv_total + jnp.dot(normed.T, qkv_grad, preferred_element_type=jnp.float32)
        out_total = out_total + jnp.dot(mixed.T, out_grad, preferred_element_type=jnp.float32)
        norm_grad = jnp.dot(qkv_grad, qkv_weight.T, preferred_element_type=jnp.float32)
        mean_one = lax.optimization_barrier(jnp.mean(norm_grad, axis=-1, keepdims=True))
        mean_two = lax.optimization_barrier(jnp.mean(norm_grad * centred, axis=-1, keepdims=True))
        frame_grad = ((norm_grad - mean_one - centred * mean_two) * inv_std).astype(jnp.bfloat16)
        return ((qkv_total, out_total), (result, frame_grad))
    start_totals = (jnp.zeros((D, 3 * D), jnp.float32), jnp.zeros((D, D), jnp.float32))
    totals, outputs = lax.scan(one_recording, start_totals, (frames, lengths, cotangent))
    return (outputs[0], outputs[1], totals[0], totals[1])
```

```python
import functools
import itertools
import math

import jax
import jax.numpy as jnp
from jax import lax
from jax.experimental import pallas as pl
from jax.experimental.pallas import tpu as pltpu
from jax.sharding import Mesh, PartitionSpec as P

H = 16
E = 64
D = 1024
GROUP = 16
LEFT = 64
AHEAD = 4
FR = 128
GF = 4 * FR
LK = 80
LQ = 16
RQ = 64
RK = 80
NK = LK + GF + RK
NQ = LQ + GF + RQ
SLAB = 2048
SIZES = {"z": 8, "yh": 2, "x": 4, "yl": 2, "c": 2}
ALL = ("z", "yh", "x", "yl", "c")
DP = ("z", "yh")
SEQ = ("x", "yl", "c")
BLOCKS = [(48 * i, 48, 48 * i) for i in range(12)] + [(576, 16, 544)]
KB = 128


def move(value, axes, target):
    sizes = [SIZES[a] for a in axes]
    pairs = []
    for coords in itertools.product(*[range(s) for s in sizes]):
        to = target(*coords)
        if to is None:
            continue
        source, dest = 0, 0
        for s, a, b in zip(sizes, coords, to):
            source, dest = source * s + a, dest * s + b
        pairs.append((source, dest))
    return lax.ppermute(value, axes if len(axes) > 1 else axes[0], pairs)


def swap_core(value):
    return move(value, ("c",), lambda c: (1 - c,))


def swap_y(value):
    return move(value, ("yl",), lambda y: (1 - y,))


def along_x(value, steps):
    return move(value, ("x",), lambda x: ((x + steps) % 4,))


def transposed(value):
    def target(z, yh, x, yl, c):
        d, s = z * 2 + yh, (x * 2 + yl) * 2 + c
        return (s // 2, s % 2, d // 4, (d // 2) % 2, d % 2)

    return move(value, ALL, target)


def nt(a, b):
    return lax.dot_general(a, b, (((1,), (1,)), ((), ())), preferred_element_type=jnp.float32)


def tn(a, b):
    return lax.dot_general(a, b, (((0,), (0,)), ((), ())), preferred_element_type=jnp.float32)


def nn(a, b):
    return jnp.dot(a, b, preferred_element_type=jnp.float32)


def piece_kernel(scal, x_ref, og_ref, w_ref, act_ref, g_ref, q_s, k_s, v_s, mg_s, o_s, dq_s, dk_s, dv_s, g_s):
    rec = pl.program_id(0)
    base = scal[0]
    length = scal[1 + rec]
    scale = 1.0 / math.sqrt(E)
    qkv = nn(x_ref[0], w_ref[:, : 3 * E]).astype(jnp.bfloat16)
    q_s[...] = qkv[:, :E]
    k_s[...] = qkv[:, E : 2 * E]
    v_s[...] = qkv[:, 2 * E :]
    mg_s[...] = nn(og_ref[0], w_ref[:, 3 * E :]).astype(jnp.bfloat16)
    dk_s[...] = jnp.zeros_like(dk_s)
    dv_s[...] = jnp.zeros_like(dv_s)
    for q0, qn, k0 in BLOCKS:
        q = q_s[LK - LQ + q0 : LK - LQ + q0 + qn, :]
        k = k_s[k0 : k0 + KB, :]
        v = v_s[k0 : k0 + KB, :]
        dy = mg_s[q0 : q0 + qn, :]
        row = lax.broadcasted_iota(jnp.int32, (qn, KB), 0)
        col = lax.broadcasted_iota(jnp.int32, (qn, KB), 1)
        q_rel = row + (q0 - LQ)
        k_rel = col + (k0 - LK)
        c_rel = (row // GROUP) * GROUP + (q0 - LQ)
        k_pos = k_rel + base
        mask = (k_rel >= c_rel - LEFT) & (k_rel < c_rel + GROUP + AHEAD)
        mask = mask & (k_pos >= 0) & (k_pos < SLAB)
        mask = mask & ((k_pos < length) | (q_rel + base >= length))
        s = jnp.where(mask, nt(q, k) * scale, -1e30)
        top = jnp.max(s, axis=-1, keepdims=True)
        e = jnp.where(mask, jnp.exp(s - top), 0.0)
        p = e * (1.0 / jnp.sum(e, axis=-1, keepdims=True))
        ph = p.astype(jnp.bfloat16)
        o_s[q0 : q0 + qn, :] = nn(ph, v).astype(jnp.bfloat16)
        dp = nt(dy, v)
        ds = p * (dp - jnp.sum(p * dp, axis=-1, keepdims=True)) * scale
        ds = ds.astype(jnp.bfloat16)
        dq_s[q0 : q0 + qn, :] = nn(ds, k).astype(jnp.bfloat16)
        dk_s[k0 : k0 + KB, :] += tn(ds, q)
        dv_s[k0 : k0 + KB, :] += tn(ph, dy)
    dqkv = jnp.concatenate(
        [
            dq_s[LQ : LQ + GF, :],
            dk_s[LK : LK + GF, :].astype(jnp.bfloat16),
            dv_s[LK : LK + GF, :].astype(jnp.bfloat16),
        ],
        axis=1,
    )
    o = o_s[LQ : LQ + GF, :]
    act_ref[0, :, : 3 * E] = dqkv
    act_ref[0, :, 3 * E :] = o
    gq = tn(dqkv, x_ref[0, LK : LK + GF, :])
    go = tn(o, og_ref[0, LQ : LQ + GF, :])

    @pl.when(rec == 0)
    def _():
        g_s[: 3 * E, :] = gq
        g_s[3 * E :, :] = go

    @pl.when(rec == 1)
    def _():
        g_ref[: 3 * E, :] = (g_s[: 3 * E, :] + gq).astype(g_ref.dtype)
        g_ref[3 * E :, :] = (g_s[3 * E :, :] + go).astype(g_ref.dtype)


def piece(scal, normed, og, w):
    return pl.pallas_call(
        piece_kernel,
        grid_spec=pltpu.PrefetchScalarGridSpec(
            num_scalar_prefetch=1,
            grid=(2,),
            in_specs=[
                pl.BlockSpec((1, NK, D), lambda r, s: (r, 0, 0)),
                pl.BlockSpec((1, NQ, D), lambda r, s: (r, 0, 0)),
                pl.BlockSpec((D, 4 * E), lambda r, s: (0, 0)),
            ],
            out_specs=[
                pl.BlockSpec((1, GF, 4 * E), lambda r, s: (r, 0, 0)),
                pl.BlockSpec((4 * E, D), lambda r, s: (0, 0)),
            ],
            scratch_shapes=[
                pltpu.VMEM((NK, E), jnp.bfloat16),
                pltpu.VMEM((NK, E), jnp.bfloat16),
                pltpu.VMEM((NK, E), jnp.bfloat16),
                pltpu.VMEM((NQ, E), jnp.bfloat16),
                pltpu.VMEM((NQ, E), jnp.bfloat16),
                pltpu.VMEM((NQ, E), jnp.bfloat16),
                pltpu.VMEM((NK, E), jnp.float32),
                pltpu.VMEM((NK, E), jnp.float32),
                pltpu.VMEM((4 * E, D), jnp.float32),
            ],
        ),
        out_shape=[
            jax.ShapeDtypeStruct((2, GF, 4 * E), jnp.bfloat16),
            jax.ShapeDtypeStruct((4 * E, D), jnp.bfloat16),
        ],
        cost_estimate=pl.CostEstimate(flops=2 * 10**9, bytes_accessed=6 * 10**6, transcendentals=10**5),
        name="piece",
    )(scal, normed, og, w)


def close_kernel(scal, a0, a1, a2, a3, w0, w1, w2, w3, ng_ref, res_ref):
    acts, ws = (a0, a1, a2, a3), (w0, w1, w2, w3)
    for rec in range(2):
        ng = sum(nt(a[rec, :, : 3 * E], w[:, : 3 * E]) for a, w in zip(acts, ws))
        res = sum(nt(a[rec, :, 3 * E :], w[:, 3 * E :]) for a, w in zip(acts, ws))
        ng_ref[0, rec] = ng.astype(ng_ref.dtype)
        res_ref[0, rec] = res.astype(res_ref.dtype)


def close(own, acts, ws):
    return pl.pallas_call(
        close_kernel,
        grid_spec=pltpu.PrefetchScalarGridSpec(
            num_scalar_prefetch=1,
            grid=(4,),
            in_specs=[pl.BlockSpec((2, FR, 4 * E), lambda j, s: (0, j ^ s[0], 0))] * 4
            + [pl.BlockSpec((D, 4 * E), lambda j, s: (0, 0))] * 4,
            out_specs=[pl.BlockSpec((1, 2, FR, D), lambda j, s: (j, 0, 0, 0))] * 2,
        ),
        out_shape=[jax.ShapeDtypeStruct((4, 2, FR, D), jnp.bfloat16)] * 2,
        cost_estimate=pl.CostEstimate(flops=2 * 10**9, bytes_accessed=6 * 10**6, transcendentals=0),
        name="close",
    )(own, *acts, *ws)


def norm_rows(frames):
    as_float = frames.astype(jnp.float32)
    row_mean = jnp.mean(as_float, axis=-1, keepdims=True)
    centred = as_float - row_mean
    variance = jnp.mean(centred * centred, axis=-1, keepdims=True)
    inv_std = lax.rsqrt(variance + 1e-05)
    return (centred * inv_std, inv_std)


def gather_group(value, own):
    other = swap_y(value)
    parts = jnp.stack([value, swap_core(value), other, swap_core(other)])
    return [lax.dynamic_index_in_dim(parts, q ^ own, 0, keepdims=False) for q in range(4)]


def sum_group(parts):
    arrived = swap_core(jnp.stack([parts[1], parts[3]]))
    near = parts[0].astype(jnp.float32) + arrived[0].astype(jnp.float32)
    far = parts[2].astype(jnp.float32) + arrived[1].astype(jnp.float32)
    return near + swap_y(far.astype(jnp.bfloat16)).astype(jnp.float32)


def halos(frames, cotangent, core, own):
    last = jnp.concatenate([frames[:, FR - LK :], cotangent[:, FR - RQ :]], axis=1)
    first = jnp.concatenate([frames[:, :RK], cotangent[:, :RQ]], axis=1)
    edge = jnp.where(core == 1, last, first)

    def by_x(x, y, c):
        if (y, c) == (1, 1) and x < 3:
            return (x + 1, 1, 1)
        if (y, c) == (0, 0) and x > 0:
            return (x - 1, 0, 0)
        return None

    def by_y(y, c):
        if (y, c) == (1, 1):
            return (0, 1)
        if (y, c) == (0, 0):
            return (1, 0)
        return None

    hop = move(edge, SEQ, by_x)
    turn = move(hop, ("yl", "c"), by_y)
    mine = jnp.where((own == 0) | (own == 3), hop, turn)
    theirs = swap_core(mine)
    left = jnp.where(core == 1, mine, theirs)
    right = jnp.where(core == 1, theirs, mine)
    return left, right


def head_columns(weight, head):
    pair = lax.dynamic_slice_in_dim(weight, (head // 2) * 128, 128, 1)
    return jnp.where(head % 2 == 0, pair[:, :E], pair[:, E:])


def per_device(frames, lengths, qkv_weight, out_weight, cotangent):
    x_index = lax.axis_index("x")
    core = lax.axis_index("c")
    own = lax.axis_index("yl") * 2 + core
    head = x_index * 4 + own
    base = x_index * GF

    shard = jnp.concatenate(
        [head_columns(qkv_weight[:, i * D : (i + 1) * D], head) for i in range(3)], axis=1
    )
    gathered = lax.all_to_all(jnp.broadcast_to(shard[None], (16, E, 3 * E)), DP, 0, 0)
    out_rows = transposed(out_weight)
    w_own = jnp.concatenate([gathered.reshape(D, 3 * E), out_rows.T], axis=1)
    w_next = along_x(w_own, -1)
    w_prev = along_x(w_own, 1)
    w_far = jnp.concatenate([along_x(w_next[: D // 2], -1), along_x(w_prev[D // 2 :], 1)], axis=0)
    ws = [w_own, w_next, w_prev, w_far]

    left, right = halos(frames, cotangent, core, own)
    frame_parts = gather_group(frames, own)
    all_frames = jnp.concatenate([left[:, :LK]] + frame_parts + [right[:, :RK]], axis=1)
    normed = norm_rows(all_frames)[0].astype(jnp.bfloat16)
    cot_parts = gather_group(cotangent, own)
    all_cot = jnp.concatenate([left[:, LK + RQ - LQ :]] + cot_parts + [right[:, RK:]], axis=1)
    query_pos = base - LQ + jnp.arange(NQ, dtype=jnp.int32)
    valid = (query_pos[None, :] < lengths[:, None])[:, :, None]
    out_grad = jnp.where(valid, all_cot, jnp.zeros_like(all_cot))

    scal = jnp.concatenate([base[None].astype(jnp.int32), lengths])
    done = [piece(scal, normed, out_grad, w) for w in ws]
    acts = [a for a, _ in done]
    g_own, g_next, g_prev, g_far = [g for _, g in done]

    from_prev = along_x(g_next, 1)
    from_next = along_x(g_prev, -1)
    far_a = along_x(along_x(g_far[: 2 * E], 1), 1)
    far_b = along_x(along_x(g_far[2 * E :], -1), -1)
    far = jnp.concatenate([far_a, far_b], axis=0)
    f32 = jnp.float32
    total = g_own.astype(f32) + from_prev.astype(f32) + from_next.astype(f32) + far.astype(f32)
    total = total.astype(jnp.bfloat16).T.reshape(16, E, 4 * E)
    spread = lax.all_to_all(total, DP, 0, 0)
    mine = jnp.sum(spread.astype(f32), axis=0).astype(jnp.bfloat16)
    out_block = transposed(mine[:, 3 * E :].T)
    final = jnp.concatenate([mine[:, : 3 * E], out_block], axis=1)
    full = lax.all_to_all(jnp.broadcast_to(final[None], (16, E, 4 * E)), SEQ, 0, 0)
    qkv_weight_grad = (
        full[:, :, : 3 * E].reshape(H, E, 3, E).transpose(1, 2, 0, 3).reshape(E, 3 * D).astype(f32)
    )
    out_weight_grad = full[:, :, 3 * E :].transpose(1, 0, 2).reshape(E, D).astype(f32)

    ng, res = close(own[None].astype(jnp.int32), acts, ws)
    projected = sum_group(res)
    own_pos = base + own * FR + jnp.arange(FR, dtype=jnp.int32)
    own_valid = (own_pos[None, :] < lengths[:, None])[:, :, None]
    result = jnp.where(own_valid, projected, 0.0).astype(jnp.bfloat16)
    norm_grad = sum_group(ng)
    centred, inv_std = norm_rows(frames)
    mean_one = jnp.mean(norm_grad, axis=-1, keepdims=True)
    mean_two = jnp.mean(norm_grad * centred, axis=-1, keepdims=True)
    frame_grad = ((norm_grad - mean_one - centred * mean_two) * inv_std).astype(jnp.bfloat16)
    return (result, frame_grad, qkv_weight_grad, out_weight_grad)


def solution(mesh):
    fine = Mesh(mesh.devices.reshape(tuple(SIZES[a] for a in ALL)), ALL)
    in_specs = (P(DP, SEQ, None), P(DP), P(DP, None), P(DP, None), P(DP, SEQ, None))
    out_specs = (P(DP, SEQ, None), P(DP, SEQ, None), P(DP, None), P(DP, None))
    return jax.shard_map(
        per_device, mesh=fine, in_specs=in_specs, out_specs=out_specs, check_vma=False
    )
```
